512 devices in a mesh: grp: 16 (over z), shard: 32 (over y, x, core).
Axes of the slice: x: 4, y: 4, z: 16, core: 2. Of those that a mesh axis runs over, the one named last changes fastest.
Arguments:
- activations: bfloat16 [1024, 5120], P('grp', 'shard'), may hold values from -6 to 6
- grad_outputs: bfloat16 [1024, 27648], P('shard', 'grp'), may hold values from -6 to 6
- basis_in: bfloat16 [5120, 2560], P('shard', 'grp'), may hold values from -0.078125 to 0.078125
- basis_out: bfloat16 [27648, 13824], P('grp', 'shard'), may hold values from -0.0390625 to 0.0390625
- query_grads: bfloat16 [16, 2560, 13824], P('grp', None, 'shard'), may hold values from -0.0009765625 to 0.0009765625
Outputs:
- scores: float32 [16, 1024], P('grp', 'shard')
The draws below stay inside these ranges and needn't reach their ends.
All inputs are finite; a program needn't handle non-finite values.
Results may differ from the reference program's by a relative error of at most 0.0041.
Values may be sent and summed in bfloat16 or wider, within the bound.
No kernel may reach another device: no remote copies, remote signals or barrier semaphores. Data moves between devices by JAX's collectives and lax.ppermute only.
A program may use at most 64 MiB of HBM per device.

```python
import jax
import jax.numpy as jnp
from jax import lax

DIN = 5120
DOUT = 27648
EIG_IN = 2560
EIG_OUT = 13824
TOKENS = 1024
N_GRP = 16


def with_spikes(result, key, source, target, blocks, factor):
    owner, partner = [(jnp.arange(result.shape[position]) // (result.shape[position] // blocks)).reshape([-1 if axis == position else 1 for axis in range(result.ndim)]) for position in (source, target)]
    chosen = jax.random.permutation(key, blocks)[partner]
    strong = (owner == chosen) | (owner == (partner + blocks // 2) % blocks)
    return jnp.where(strong, factor * result, result)


def shard_levels(key, shape, pieces, least, top_value):
    gain = 1.0
    for axis_at, shards_of in pieces:
        draws = jax.random.uniform(jax.random.fold_in(jax.random.fold_in(key, 6), axis_at), (shards_of,), jnp.float32, least / len(pieces), top_value / len(pieces))
        gain = gain * jnp.repeat(jnp.exp(draws), shape[axis_at] // shards_of).reshape((-1,) + (1,) * (len(shape) - 1 - axis_at))
    return gain


def gaussian(rng, extent, deviation, reach, shards=(), dtype=jnp.bfloat16):
    drawn = jax.random.normal(rng, extent, jnp.float32) * deviation
    if len(shards) > 0:
        drawn = shard_levels(rng, extent, shards, -0.22, 0.18) * drawn
    return jnp.clip(drawn, min=-reach, max=reach).astype(dtype)


def noise_with(stream_key, shape, spread, limit, shards, heavy, dtype=jnp.bfloat16):
    drawn = spread * jax.random.normal(stream_key, shape, jnp.float32)
    if shards:
        drawn = drawn * shard_levels(stream_key, shape, shards, -0.22, 0.18)
    return jnp.clip(with_spikes(drawn, jax.random.fold_in(stream_key, 3), *heavy), -limit, limit).astype(dtype)


def setup_inputs(seed: int = 0) -> dict:
    keys = jax.random.split(jax.random.key(seed), 6)
    return {
        "activations": gaussian(keys[0], (TOKENS, DIN), 1.0, 6.0, ((0, 16), (1, 32))),
        "grad_outputs": noise_with(keys[1], (TOKENS, DOUT), 1.0, 6.0, ((0, 32), (1, 16)), (1, 0, 32, 2.75)),
        "basis_in": gaussian(keys[2], (DIN, EIG_IN), DIN ** -0.5, 0.078125, ((0, 32), (1, 16))),
        "basis_out": gaussian(keys[3], (DOUT, EIG_OUT), DOUT ** -0.5, 0.0390625, ((0, 16), (1, 32))),
        "query_grads": gaussian(keys[4], (N_GRP, EIG_IN, EIG_OUT), (EIG_IN * EIG_OUT) ** -0.5, 0.0009765625, ((0, 16), (2, 32))),
    }


def reference(activations, grad_outputs, basis_in, basis_out, query_grads):
    act_rot = jnp.dot(activations, basis_in, preferred_element_type=jnp.float32).astype(jnp.bfloat16)
    out_rot = jnp.dot(grad_outputs, basis_out, preferred_element_type=jnp.float32).astype(jnp.bfloat16)
    out_wide = out_rot.astype(jnp.float32)

    def one_query(query):
        mixed = jnp.dot(act_rot, query, preferred_element_type=jnp.float32)
        return jnp.sum(mixed * out_wide, axis=1)

    return lax.map(one_query, query_grads)
```

```python
import jax
import jax.numpy as jnp
from jax import lax
from jax.sharding import PartitionSpec as P


F32 = jnp.float32
BF16 = jnp.bfloat16
NT = (((1,), (1,)), ((), ()))


def product(left, right):
    return lax.dot_general(left, right, NT, preferred_element_type=F32)


def spread(block, axis, count, groups):
    copies = jnp.broadcast_to(block[None], (count, *block.shape))
    return lax.all_to_all(copies, axis, 0, 0, axis_index_groups=groups)


def local(activations, grad_outputs, basis_in, basis_out, query_grads):
    n_grp = lax.axis_size("grp")
    n_shard = lax.axis_size("shard")
    chips = n_shard // 2
    one_core = [[2 * chip + core for chip in range(chips)] for core in range(2)]
    other_core = [(at, at ^ 1) for at in range(n_shard)]
    pairs = [(at, at ^ 1) for at in range(n_grp)]
    cross_pairs = [(at, (at + (1 if at % 2 else -1)) % n_grp) for at in range(n_grp)]
    alike = [list(range(parity, n_grp, 2)) for parity in range(2)]
    rows = grad_outputs.shape[0]
    half = chips * rows
    eig = basis_in.shape[1]
    parity = lax.axis_index("grp") % 2

    grads = spread(grad_outputs, "shard", chips, one_core)
    basis_own = basis_out.T
    basis_other = lax.ppermute(basis_own, "shard", other_core)
    query_own = query_grads[0].T
    query_other = lax.ppermute(query_own, "shard", other_core)
    acts = lax.all_gather(activations, "grp", axis=0, tiled=True)

    act_terms = jnp.dot(acts, basis_in, preferred_element_type=F32)
    act_terms = lax.all_to_all(act_terms.reshape(n_shard, rows, eig), "shard", 0, 0)
    act_own = jnp.sum(act_terms, axis=0).astype(BF16)

    grads = grads.reshape(n_grp // 2, 2, rows, -1)
    passed = lax.dynamic_index_in_dim(grads, 1 - parity, 1, keepdims=False).reshape(half // 2, -1)
    passed_own = product(passed, basis_own).astype(BF16)
    passed_other = product(passed, basis_other).astype(BF16)
    got_own = lax.ppermute(passed_own, "grp", pairs)
    got_other = lax.ppermute(passed_other, "grp", cross_pairs)
    kept = lax.dynamic_index_in_dim(grads, parity, 1, keepdims=False).reshape(half // 2, -1)
    kept_own = product(kept, basis_own) + got_own.astype(F32)
    kept_other = product(kept, basis_other) + got_other.astype(F32)
    out_terms = jnp.concatenate([kept_own, kept_other], axis=1).astype(BF16)
    out_terms = lax.all_to_all(
        out_terms.reshape(n_grp // 2, rows, -1), "grp", 0, 0, axis_index_groups=alike
    )
    out_own = jnp.sum(out_terms.astype(F32), axis=0).astype(BF16)

    act_cols = lax.all_gather(act_own, "grp", axis=0, tiled=False)
    act_rot = act_cols.transpose(1, 0, 2).reshape(rows, n_grp * eig)
    act_rot = spread(act_rot, "shard", chips, one_core).reshape(half, n_grp * eig)
    out_rot = lax.all_gather(out_own, "grp", axis=0, tiled=True)

    query = jnp.concatenate([query_own, query_other], axis=0)
    partial = jnp.sum(product(act_rot, query) * out_rot.astype(F32), axis=1)
    partial = jnp.broadcast_to(partial.reshape(chips, 1, rows), (chips, 8, rows))
    partial = lax.all_to_all(partial, "shard", 0, 0, axis_index_groups=one_core)
    return jnp.sum(partial[:, :1], axis=0)


def solution(mesh):
    placed = (
        P("grp", "shard"),
        P("shard", "grp"),
        P("shard", "grp"),
        P("grp", "shard"),
        P("grp", None, "shard"),
    )
    return jax.shard_map(
        local, mesh=mesh, in_specs=placed, out_specs=P("grp", "shard"), check_vma=False
    )
```

```python
import functools

import jax
import jax.numpy as jnp
from jax import lax
from jax.experimental import pallas as pl
from jax.experimental.pallas import tpu as pltpu
from jax.sharding import PartitionSpec as P


F32 = jnp.float32
BF16 = jnp.bfloat16
NT = (((1,), (1,)), ((), ()))


def product(left, right):
    return lax.dot_general(left, right, NT, preferred_element_type=F32)


def spread(block, axis, count, groups):
    copies = jnp.broadcast_to(block[None], (count, *block.shape))
    return lax.all_to_all(copies, axis, 0, 0, axis_index_groups=groups)


CUT = 512


def terms_kernel(quads, few, parity_ref, grads_ref, own_hbm, other_hbm, keep_ref, low_ref, high_ref, basis, terms, sems):
    cols = own_hbm.shape[0]
    first = pltpu.make_async_copy(own_hbm, basis.at[:cols], sems.at[0])
    second = pltpu.make_async_copy(other_hbm, basis.at[cols:], sems.at[1])
    first.start()
    second.start()
    first.wait()
    second.wait()
    terms[...] = product(grads_ref[...], basis[...])
    parity = parity_ref[0]
    for block in range(2 * quads):
        quad, pair = block // 2, block % 2

        def rows_of(which):
            rows = []
            for at in range(4):
                start = ((quad * 4 + at) * 4 + pair * 2) * few
                rows.append(terms[pl.ds(pl.multiple_of(start + which * few, few), few), :])
            return jnp.concatenate(rows, axis=0)

        keep_ref[block] = rows_of(parity)
        passed = rows_of(1 - parity).astype(BF16)
        low_ref[block] = passed[:, :CUT]
        high_ref[block] = passed[:, CUT:]


def out_terms(parity, grads, own, other, quads, few):
    blocks, rows, cols = 2 * quads, 4 * few, 2 * own.shape[0]
    smem, vmem = pl.BlockSpec(memory_space=pltpu.SMEM), pl.BlockSpec(memory_space=pltpu.VMEM)
    hbm = pl.BlockSpec(memory_space=pl.ANY)
    flops = 2 * grads.shape[0] * grads.shape[1] * cols
    return pl.pallas_call(
        functools.partial(terms_kernel, quads, few),
        out_shape=(
            jax.ShapeDtypeStruct((blocks, rows, cols), F32),
            jax.ShapeDtypeStruct((blocks, rows, CUT), BF16),
            jax.ShapeDtypeStruct((blocks, rows, cols - CUT), BF16),
        ),
        in_specs=[smem, vmem, hbm, hbm],
        out_specs=(vmem, vmem, vmem),
        scratch_shapes=[
            pltpu.VMEM((cols, grads.shape[1]), BF16),
            pltpu.VMEM((grads.shape[0], cols), F32),
            pltpu.SemaphoreType.DMA((2,)),
        ],
        cost_estimate=pl.CostEstimate(flops=flops, bytes_accessed=6 << 20, transcendentals=0),
        name="out_terms",
    )(parity, grads, own, other)


def message_kernel(wide, parity_ref, keep_ref, low_ref, high_ref, own_ref, near_ref, sent_ref):
    odd = parity_ref[0] == 1
    own, near = own_ref[...].astype(F32), near_ref[...].astype(F32)
    act = jnp.concatenate([jnp.where(odd, near, own), jnp.where(odd, own, near)], axis=0)
    rest = act[:, wide:]
    blank = jnp.zeros((act.shape[0], 2 * wide - act.shape[1]), F32)
    act = jnp.concatenate([act[:, :wide], jnp.concatenate([rest, blank], axis=1)], axis=0)
    act = act.astype(BF16)
    for block in range(keep_ref.shape[0]):
        sent_ref[block, :, :wide] = act
        low = keep_ref[block, :, :CUT] + low_ref[block].astype(F32)
        sent_ref[block, :, wide : wide + CUT] = low.astype(BF16)
        high = keep_ref[block, :, CUT:] + high_ref[block].astype(F32)
        sent_ref[block, :, wide + CUT :] = high.astype(BF16)


def message(parity, keep, low, high, own, near, wide):
    smem, vmem = pl.BlockSpec(memory_space=pltpu.SMEM), pl.BlockSpec(memory_space=pltpu.VMEM)
    shape = (*keep.shape[:2], wide + keep.shape[2])
    return pl.pallas_call(
        functools.partial(message_kernel, wide),
        out_shape=jax.ShapeDtypeStruct(shape, BF16),
        in_specs=[smem] + [vmem] * 5,
        out_specs=vmem,
        cost_estimate=pl.CostEstimate(flops=1 << 20, bytes_accessed=2 << 20, transcendentals=0),
        name="message",
    )(parity, keep, low, high, own, near)


def local(activations, grad_outputs, basis_in, basis_out, query_grads):
    n_grp = lax.axis_size("grp")
    n_shard = lax.axis_size("shard")
    chips = n_shard // 2
    one_core = [[2 * chip + core for chip in range(chips)] for core in range(2)]
    other_core = [(at, at ^ 1) for at in range(n_shard)]
    pairs = [(at, at ^ 1) for at in range(n_grp)]
    cross_pairs = [(at, (at + (1 if at % 2 else -1)) % n_grp) for at in range(n_grp)]
    alike = [list(range(parity, n_grp, 2)) for parity in range(2)]
    quads = n_grp // 4
    far = [list(range(at, n_grp, 4)) for at in range(4)]
    rows = grad_outputs.shape[0]
    few = rows // 4
    half = chips * rows
    eig = 4 * basis_in.shape[1]
    place = lax.axis_index("grp")
    parity = place & 1

    grads = spread(grad_outputs, "shard", chips, one_core).reshape(half, -1)
    basis_own = basis_out.T
    basis_other = lax.ppermute(basis_own, "shard", other_core)
    query_own = query_grads[0].T
    query_other = lax.ppermute(query_own, "shard", other_core)

    near = [basis_in]
    for at in range(1, 4):
        near.append(lax.ppermute(basis_in, "grp", [(to, to ^ at) for to in range(n_grp)]))
    odd = parity == 1
    near = [jnp.where(odd, near[at ^ 1], near[at]) for at in range(4)]
    late = (place & 2) == 2
    near = [jnp.where(late, near[at ^ 2], near[at]) for at in range(4)]
    basis = jnp.concatenate(near, axis=1)
    acts = activations.reshape(2, 4, few, -1).transpose(1, 0, 2, 3).reshape(2 * rows, -1)
    acts = lax.all_gather(acts, "grp", axis=0, tiled=True, axis_index_groups=far)
    act_terms = jnp.dot(acts, basis, preferred_element_type=F32)
    act_terms = lax.all_to_all(act_terms.reshape(n_shard, few, eig), "shard", 0, 0)
    act_own = jnp.sum(act_terms, axis=0).astype(BF16)
    act_near = lax.ppermute(act_own, "grp", pairs)

    parity_at = parity.astype(jnp.int32).reshape(1)
    keep, low, high = out_terms(parity_at, grads, basis_own, basis_other, quads, few)
    low = lax.ppermute(low, "grp", pairs)
    high = lax.ppermute(high, "grp", cross_pairs)

    wide = -(-eig // 256) * 128
    skip = 2 * wide - eig
    sent = message(parity_at, keep, low, high, act_own, act_near, wide)
    got = lax.all_to_all(sent, "grp", 0, 0, axis_index_groups=alike)
    out_own = jnp.sum(got[:, :, wide:].astype(F32), axis=0).astype(BF16)
    act_rot = jnp.concatenate([got[:, : 2 * few, :wide], got[:, 2 * few :, : wide - skip]], axis=2)
    act_rot = act_rot.reshape(quads, 2, 2 * few, eig).transpose(1, 2, 0, 3)
    act_rot = act_rot.reshape(rows, quads * eig)
    act_rot = spread(act_rot, "shard", chips, one_core).reshape(half, quads * eig)
    out_rot = lax.all_gather(out_own, "grp", axis=0, tiled=True)

    query = jnp.concatenate([query_own, query_other], axis=0)
    partial = jnp.sum(product(act_rot, query) * out_rot.astype(F32), axis=1)
    partial = partial.reshape(quads, 4, 4, few).transpose(0, 2, 1, 3).reshape(chips, 1, rows)
    partial = jnp.pad(partial, ((0, 0), (0, 7), (0, 128 - rows)))
    partial = lax.all_to_all(partial, "shard", 0, 0, axis_index_groups=one_core)
    return jnp.sum(partial, axis=0)[:1, :rows]


def solution(mesh):
    placed = (
        P("grp", "shard"),
        P("shard", "grp"),
        P("shard", "grp"),
        P("grp", "shard"),
        P("grp", None, "shard"),
    )
    return jax.shard_map(
        local, mesh=mesh, in_specs=placed, out_specs=P("grp", "shard"), check_vma=False
    )
```

```python
import functools

import jax
import jax.numpy as jnp
from jax import lax
from jax.experimental import pallas as pl
from jax.experimental.pallas import tpu as pltpu
from jax.sharding import PartitionSpec as P


F32 = jnp.float32
BF16 = jnp.bfloat16
NT = (((1,), (1,)), ((), ()))


def product(left, right):
    return lax.dot_general(left, right, NT, preferred_element_type=F32)


def spread(block, axis, count, groups):
    copies = jnp.broadcast_to(block[None], (count, *block.shape))
    return lax.all_to_all(copies, axis, 0, 0, axis_index_groups=groups)


CUT = 512


def terms_kernel(quads, few, parity_ref, grads_ref, own_hbm, other_hbm, keep_ref, low_ref, high_ref, basis, sems):
    cols = own_hbm.shape[0]
    first = pltpu.make_async_copy(own_hbm, basis.at[:cols], sems.at[0])
    second = pltpu.make_async_copy(other_hbm, basis.at[cols:], sems.at[1])
    first.start()
    second.start()
    odd = parity_ref[0] == 1

    def put(start, stop):
        terms = product(grads_ref[...], basis[start:stop])
        for block in range(2 * quads):
            quad, pair = block // 2, block % 2
            halves = []
            for which in range(2):
                begins = [((quad * 4 + at) * 4 + pair * 2 + which) * few for at in range(4)]
                halves.append(jnp.concatenate([terms[at : at + few] for at in begins], axis=0))
            keep_ref[block, :, start:stop] = jnp.where(odd, halves[1], halves[0])
            passed = jnp.where(odd, halves[0], halves[1]).astype(BF16)
            if stop <= CUT:
                low_ref[block, :, start:stop] = passed
            else:
                high_ref[block, :, start - CUT : stop - CUT] = passed

    first.wait()
    put(0, 384)
    second.wait()
    put(384, CUT)
    put(CUT, 2 * cols)


def out_terms(parity, grads, own, other, quads, few):
    blocks, rows, cols = 2 * quads, 4 * few, 2 * own.shape[0]
    smem, vmem = pl.BlockSpec(memory_space=pltpu.SMEM), pl.BlockSpec(memory_space=pltpu.VMEM)
    hbm = pl.BlockSpec(memory_space=pl.ANY)
    flops = 2 * grads.shape[0] * grads.shape[1] * cols
    return pl.pallas_call(
        functools.partial(terms_kernel, quads, few),
        out_shape=(
            jax.ShapeDtypeStruct((blocks, rows, cols), F32),
            jax.ShapeDtypeStruct((blocks, rows, CUT), BF16),
            jax.ShapeDtypeStruct((blocks, rows, cols - CUT), BF16),
        ),
        in_specs=[smem, vmem, hbm, hbm],
        out_specs=(vmem, vmem, vmem),
        scratch_shapes=[
            pltpu.VMEM((cols, grads.shape[1]), BF16),
            pltpu.SemaphoreType.DMA((2,)),
        ],
        cost_estimate=pl.CostEstimate(flops=flops, bytes_accessed=6 << 20, transcendentals=0),
        name="out_terms",
    )(parity, grads, own, other)


def message_kernel(wide, parity_ref, keep_ref, low_ref, high_ref, own_ref, near_ref, sent_ref):
    odd = parity_ref[0] == 1
    own, near = own_ref[...].astype(F32), near_ref[...].astype(F32)
    act = jnp.concatenate([jnp.where(odd, near, own), jnp.where(odd, own, near)], axis=0)
    rest = act[:, wide:]
    blank = jnp.zeros((act.shape[0], 2 * wide - act.shape[1]), F32)
    act = jnp.concatenate([act[:, :wide], jnp.concatenate([rest, blank], axis=1)], axis=0)
    act = act.astype(BF16)
    for block in range(keep_ref.shape[0]):
        sent_ref[block, :, :wide] = act
        low = keep_ref[block, :, :CUT] + low_ref[block].astype(F32)
        sent_ref[block, :, wide : wide + CUT] = low.astype(BF16)
        high = keep_ref[block, :, CUT:] + high_ref[block].astype(F32)
        sent_ref[block, :, wide + CUT :] = high.astype(BF16)


def message(parity, keep, low, high, own, near, wide):
    smem, vmem = pl.BlockSpec(memory_space=pltpu.SMEM), pl.BlockSpec(memory_space=pltpu.VMEM)
    shape = (*keep.shape[:2], wide + keep.shape[2])
    return pl.pallas_call(
        functools.partial(message_kernel, wide),
        out_shape=jax.ShapeDtypeStruct(shape, BF16),
        in_specs=[smem] + [vmem] * 5,
        out_specs=vmem,
        cost_estimate=pl.CostEstimate(flops=1 << 20, bytes_accessed=2 << 20, transcendentals=0),
        name="message",
    )(parity, keep, low, high, own, near)


def scores_kernel(quads, few, act_hbm, own_hbm, other_hbm, out_hbm, part_ref, act, query, out, sems):
    rows, cols, half = act.shape[0] // 4, query.shape[0], own_hbm.shape[0]
    blocks = [pl.ds(at * rows, rows) for at in range(4)]
    steps = [(at, min(at + 256, cols)) for at in range(0, cols, 256)]
    cuts = sorted({0, half, cols} | {at for at, _ in steps})
    loads = []
    for at, to in zip(cuts[:-1], cuts[1:], strict=True):
        source = own_hbm.at[at:to] if to <= half else other_hbm.at[at - half : to - half]
        copy = pltpu.make_async_copy(source, query.at[at:to], sems.at[len(loads)])
        loads.append((to, copy))
    acts = []
    for at, block in enumerate(blocks):
        sem = sems.at[len(loads) + at]
        acts.append(pltpu.make_async_copy(act_hbm.at[block], act.at[block], sem))
    outs = pltpu.make_async_copy(out_hbm, out, sems.at[len(loads) + 4])
    loads[0][1].start()
    for copy in (*acts, outs):
        copy.start()
    for _, copy in loads[1:]:
        copy.start()

    ready = 0
    totals = [jnp.zeros((rows, 128), F32)] * 4
    for start, stop in steps:
        while ready < len(loads) and (ready == 0 or loads[ready - 1][0] < stop):
            loads[ready][1].wait()
            ready += 1
        for at, block in enumerate(blocks):
            if start == 0:
                acts[at].wait()
            terms = product(act[block], query[start:stop])
            if start == 0 and at == 0:
                outs.wait()
            terms = terms * out[block, start:stop].astype(F32)
            for lane in range(0, stop - start, 128):
                piece = terms[:, lane : lane + 128]
                short = 128 - piece.shape[1]
                if short:
                    piece = jnp.concatenate([piece, jnp.zeros((rows, short), F32)], axis=1)
                totals[at] = totals[at] + piece

    total = jnp.concatenate(totals, axis=0)
    moved = []
    for quad in range(quads):
        for second in range(4):
            for third in range(4):
                at = ((quad * 4 + third) * 4 + second) * few
                moved.append(total[at : at + few])
    line = jnp.sum(jnp.concatenate(moved, axis=0).T, axis=0, keepdims=True)
    part_ref[...] = jnp.zeros_like(part_ref)
    for at in range(part_ref.shape[0]):
        part_ref[at, :1, : 4 * few] = line[:, at * 4 * few : (at + 1) * 4 * few]


def part_scores(act, own, other, out, quads, few):
    hbm = pl.BlockSpec(memory_space=pl.ANY)
    cols = 2 * own.shape[0]
    flops = 2 * act.shape[0] * act.shape[1] * cols
    return pl.pallas_call(
        functools.partial(scores_kernel, quads, few),
        out_shape=jax.ShapeDtypeStruct((act.shape[0] // (4 * few), 8, 128), F32),
        in_specs=[hbm] * 4,
        out_specs=pl.BlockSpec(memory_space=pltpu.VMEM),
        scratch_shapes=[
            pltpu.VMEM(act.shape, BF16),
            pltpu.VMEM((cols, act.shape[1]), BF16),
            pltpu.VMEM(out.shape, BF16),
            pltpu.SemaphoreType.DMA((10,)),
        ],
        cost_estimate=pl.CostEstimate(flops=flops, bytes_accessed=8 << 20, transcendentals=0),
        compiler_params=pltpu.CompilerParams(vmem_limit_bytes=66_000_000),
        name="part_scores",
    )(act, own, other, out)


def local(activations, grad_outputs, basis_in, basis_out, query_grads):
    n_grp = lax.axis_size("grp")
    n_shard = lax.axis_size("shard")
    chips = n_shard // 2
    one_core = [[2 * chip + core for chip in range(chips)] for core in range(2)]
    other_core = [(at, at ^ 1) for at in range(n_shard)]
    pairs = [(at, at ^ 1) for at in range(n_grp)]
    cross_pairs = [(at, (at + (1 if at % 2 else -1)) % n_grp) for at in range(n_grp)]
    alike = [list(range(parity, n_grp, 2)) for parity in range(2)]
    quads = n_grp // 4
    far = [list(range(at, n_grp, 4)) for at in range(4)]
    rows = grad_outputs.shape[0]
    few = rows // 4
    half = chips * rows
    eig = 4 * basis_in.shape[1]
    place = lax.axis_index("grp")
    parity = place & 1

    grads = spread(grad_outputs, "shard", chips, one_core).reshape(half, -1)
    basis_own = basis_out.T
    basis_other = lax.ppermute(basis_own, "shard", other_core)
    query_own = query_grads[0].T
    query_other = lax.ppermute(query_own, "shard", other_core)

    near = [basis_in]
    for at in range(1, 4):
        near.append(lax.ppermute(basis_in, "grp", [(to, to ^ at) for to in range(n_grp)]))
    odd = parity == 1
    near = [jnp.where(odd, near[at ^ 1], near[at]) for at in range(4)]
    late = (place & 2) == 2
    near = [jnp.where(late, near[at ^ 2], near[at]) for at in range(4)]
    basis = jnp.concatenate(near, axis=1)
    acts = activations.reshape(2, 4, few, -1).transpose(1, 0, 2, 3).reshape(2 * rows, -1)
    acts = lax.all_gather(acts, "grp", axis=0, tiled=True, axis_index_groups=far)
    act_terms = jnp.dot(acts, basis, preferred_element_type=F32)
    act_terms = lax.all_to_all(act_terms.reshape(n_shard, few, eig), "shard", 0, 0)
    act_own = jnp.sum(act_terms, axis=0).astype(BF16)
    act_near = lax.ppermute(act_own, "grp", pairs)

    parity_at = parity.astype(jnp.int32).reshape(1)
    keep, low, high = out_terms(parity_at, grads, basis_own, basis_other, quads, few)
    low = lax.ppermute(low, "grp", pairs)
    high = lax.ppermute(high, "grp", cross_pairs)

    wide = -(-eig // 256) * 128
    skip = 2 * wide - eig
    sent = message(parity_at, keep, low, high, act_own, act_near, wide)
    got = lax.all_to_all(sent, "grp", 0, 0, axis_index_groups=alike)
    out_own = jnp.sum(got[:, :, wide:].astype(F32), axis=0).astype(BF16)
    act_rot = jnp.concatenate([got[:, : 2 * few, :wide], got[:, 2 * few :, : wide - skip]], axis=2)
    act_rot = act_rot.reshape(quads, 2, 2 * few, eig).transpose(1, 2, 0, 3)
    act_rot = act_rot.reshape(rows, quads * eig)
    act_rot = spread(act_rot, "shard", chips, one_core).reshape(half, quads * eig)
    out_rot = lax.all_gather(out_own, "grp", axis=0, tiled=True)

    partial = part_scores(act_rot, query_own, query_other, out_rot, quads, few)
    partial = lax.all_to_all(partial, "shard", 0, 0, axis_index_groups=one_core)
    return jnp.sum(partial, axis=0)[:1, :rows]


def solution(mesh):
    placed = (
        P("grp", "shard"),
        P("shard", "grp"),
        P("shard", "grp"),
        P("grp", "shard"),
        P("grp", None, "shard"),
    )
    return jax.shard_map(
        local, mesh=mesh, in_specs=placed, out_specs=P("grp", "shard"), check_vma=False
    )
```

```python
import functools

import jax
import jax.numpy as jnp
from jax import lax
from jax.experimental import pallas as pl
from jax.experimental.pallas import tpu as pltpu
from jax.sharding import PartitionSpec as P


F32 = jnp.float32
BF16 = jnp.bfloat16
NT = (((1,), (1,)), ((), ()))


def product(left, right):
    return lax.dot_general(left, right, NT, preferred_element_type=F32)


def spread(block, axis, count, groups):
    copies = jnp.broadcast_to(block[None], (count, *block.shape))
    return lax.all_to_all(copies, axis, 0, 0, axis_index_groups=groups)


CUT = 512


def terms_kernel(quads, few, parity_ref, grads_ref, own_hbm, other_hbm, keep_ref, low_ref, high_ref, basis, terms, sems):
    cols = own_hbm.shape[0]
    first = pltpu.make_async_copy(own_hbm, basis.at[:cols], sems.at[0])
    second = pltpu.make_async_copy(other_hbm, basis.at[cols:], sems.at[1])
    first.start()
    second.start()
    first.wait()
    second.wait()
    terms[...] = product(grads_ref[...], basis[...])
    parity = parity_ref[0]
    for block in range(2 * quads):
        quad, pair = block // 2, block % 2

        def rows_of(which):
            rows = []
            for at in range(4):
                start = ((quad * 4 + at) * 4 + pair * 2) * few
                rows.append(terms[pl.ds(pl.multiple_of(start + which * few, few), few), :])
            return jnp.concatenate(rows, axis=0)

        keep_ref[block] = rows_of(parity)
        passed = rows_of(1 - parity).astype(BF16)
        low_ref[block] = passed[:, :CUT]
        high_ref[block] = passed[:, CUT:]


def out_terms(parity, grads, own, other, quads, few):
    blocks, rows, cols = 2 * quads, 4 * few, 2 * own.shape[0]
    smem, vmem = pl.BlockSpec(memory_space=pltpu.SMEM), pl.BlockSpec(memory_space=pltpu.VMEM)
    hbm = pl.BlockSpec(memory_space=pl.ANY)
    flops = 2 * grads.shape[0] * grads.shape[1] * cols
    return pl.pallas_call(
        functools.partial(terms_kernel, quads, few),
        out_shape=(
            jax.ShapeDtypeStruct((blocks, rows, cols), F32),
            jax.ShapeDtypeStruct((blocks, rows, CUT), BF16),
            jax.ShapeDtypeStruct((blocks, rows, cols - CUT), BF16),
        ),
        in_specs=[smem, vmem, hbm, hbm],
        out_specs=(vmem, vmem, vmem),
        scratch_shapes=[
            pltpu.VMEM((cols, grads.shape[1]), BF16),
            pltpu.VMEM((grads.shape[0], cols), F32),
            pltpu.SemaphoreType.DMA((2,)),
        ],
        cost_estimate=pl.CostEstimate(flops=flops, bytes_accessed=6 << 20, transcendentals=0),
        name="out_terms",
    )(parity, grads, own, other)


def message_kernel(wide, parity_ref, keep_ref, low_ref, high_ref, own_ref, near_ref, sent_ref):
    odd = parity_ref[0] == 1
    own, near = own_ref[...].astype(F32), near_ref[...].astype(F32)
    act = jnp.concatenate([jnp.where(odd, near, own), jnp.where(odd, own, near)], axis=0)
    act = act.astype(BF16)
    rows, cols = act.shape[0], keep_ref.shape[2]
    blank = jnp.zeros((rows, wide - cols), BF16)
    for block in range(keep_ref.shape[0]):
        low = (keep_ref[block, :, :CUT] + low_ref[block].astype(F32)).astype(BF16)
        high = (keep_ref[block, :, CUT:] + high_ref[block].astype(F32)).astype(BF16)
        for at in range(2):
            begin, part = at * wide, slice(at * rows, (at + 1) * rows)
            sent_ref[block, :, begin : begin + CUT] = low[part]
            sent_ref[block, :, begin + CUT : begin + cols] = high[part]
            sent_ref[block, :, begin + cols : begin + wide] = blank
        sent_ref[block, :, 2 * wide :] = act


def message(parity, keep, low, high, own, near, wide):
    smem, vmem = pl.BlockSpec(memory_space=pltpu.SMEM), pl.BlockSpec(memory_space=pltpu.VMEM)
    shape = (keep.shape[0], keep.shape[1] // 2, 2 * wide + own.shape[1])
    return pl.pallas_call(
        functools.partial(message_kernel, wide),
        out_shape=jax.ShapeDtypeStruct(shape, BF16),
        in_specs=[smem] + [vmem] * 5,
        out_specs=vmem,
        cost_estimate=pl.CostEstimate(flops=1 << 20, bytes_accessed=2 << 20, transcendentals=0),
        name="message",
    )(parity, keep, low, high, own, near)


def own_kernel(wide, got_ref, out_ref):
    rows, cols = got_ref.shape[1], out_ref.shape[1]
    for at in range(2):
        total = jnp.zeros((rows, cols), F32)
        for block in range(got_ref.shape[0]):
            total = total + got_ref[block, :, at * wide : at * wide + cols].astype(F32)
        out_ref[at * rows : (at + 1) * rows] = total.astype(BF16)


def own_terms(got, cols, wide):
    vmem = pl.BlockSpec(memory_space=pltpu.VMEM)
    return pl.pallas_call(
        functools.partial(own_kernel, wide),
        out_shape=jax.ShapeDtypeStruct((2 * got.shape[1], cols), BF16),
        in_specs=[vmem],
        out_specs=vmem,
        cost_estimate=pl.CostEstimate(flops=1 << 18, bytes_accessed=1 << 19, transcendentals=0),
        name="own_terms",
    )(got)


def local(activations, grad_outputs, basis_in, basis_out, query_grads):
    n_grp = lax.axis_size("grp")
    n_shard = lax.axis_size("shard")
    chips = n_shard // 2
    one_core = [[2 * chip + core for chip in range(chips)] for core in range(2)]
    other_core = [(at, at ^ 1) for at in range(n_shard)]
    pairs = [(at, at ^ 1) for at in range(n_grp)]
    cross_pairs = [(at, (at + (1 if at % 2 else -1)) % n_grp) for at in range(n_grp)]
    alike = [list(range(parity, n_grp, 2)) for parity in range(2)]
    quads = n_grp // 4
    far = [list(range(at, n_grp, 4)) for at in range(4)]
    rows = grad_outputs.shape[0]
    few = rows // 4
    half = chips * rows
    eig = 4 * basis_in.shape[1]
    place = lax.axis_index("grp")
    parity = place & 1

    grads = spread(grad_outputs, "shard", chips, one_core).reshape(half, -1)
    basis_own = basis_out.T
    basis_other = lax.ppermute(basis_own, "shard", other_core)
    query_own = query_grads[0].T
    query_other = lax.ppermute(query_own, "shard", other_core)

    near = [basis_in]
    for at in range(1, 4):
        near.append(lax.ppermute(basis_in, "grp", [(to, to ^ at) for to in range(n_grp)]))
    odd = parity == 1
    near = [jnp.where(odd, near[at ^ 1], near[at]) for at in range(4)]
    late = (place & 2) == 2
    near = [jnp.where(late, near[at ^ 2], near[at]) for at in range(4)]
    basis = jnp.concatenate(near, axis=1)
    acts = activations.reshape(2, 4, few, -1).transpose(1, 0, 2, 3).reshape(2 * rows, -1)
    acts = lax.all_gather(acts, "grp", axis=0, tiled=True, axis_index_groups=far)
    act_terms = jnp.dot(acts, basis, preferred_element_type=F32)
    act_terms = lax.all_to_all(act_terms.reshape(n_shard, few, eig), "shard", 0, 0)
    act_own = jnp.sum(act_terms, axis=0).astype(BF16)
    act_near = lax.ppermute(act_own, "grp", pairs)

    parity_at = parity.astype(jnp.int32).reshape(1)
    keep, low, high = out_terms(parity_at, grads, basis_own, basis_other, quads, few)
    low = lax.ppermute(low, "grp", pairs)
    high = lax.ppermute(high, "grp", cross_pairs)

    cols = keep.shape[2]
    wide = -(-cols // 128) * 128
    sent = message(parity_at, keep, low, high, act_own, act_near, wide)
    got = lax.all_to_all(sent, "grp", 0, 0, axis_index_groups=alike)
    out_own = own_terms(got, cols, wide)
    act_rot = got[:, :, 2 * wide :]
    act_rot = act_rot.reshape(quads, 2, 2 * few, eig).transpose(1, 2, 0, 3)
    act_rot = act_rot.reshape(rows, quads * eig)
    act_rot = spread(act_rot, "shard", chips, one_core).reshape(half, quads * eig)
    out_rot = lax.all_gather(out_own, "grp", axis=0, tiled=True)

    query = jnp.concatenate([query_own, query_other], axis=0)
    partial = jnp.sum(product(act_rot, query) * out_rot.astype(F32), axis=1)
    partial = partial.reshape(quads, 4, 4, few).transpose(0, 2, 1, 3).reshape(chips, 1, rows)
    partial = jnp.pad(partial, ((0, 0), (0, 7), (0, 128 - rows)))
    partial = lax.all_to_all(partial, "shard", 0, 0, axis_index_groups=one_core)
    return jnp.sum(partial, axis=0)[:1, :rows]


def solution(mesh):
    placed = (
        P("grp", "shard"),
        P("shard", "grp"),
        P("shard", "grp"),
        P("grp", "shard"),
        P("grp", None, "shard"),
    )
    return jax.shard_map(
        local, mesh=mesh, in_specs=placed, out_specs=P("grp", "shard"), check_vma=False
    )
```
